32 devices in a mesh: leaf: 4 (over z), grid: 4 (over y, x), rhs: 2 (over core).
Axes of the slice: x: 2, y: 2, z: 4, core: 2. Of those that a mesh axis runs over, the one named last changes fastest.
Arguments:
- b_leaf: bfloat16 [16384, 256], P(('leaf', 'grid'), 'rhs'), may hold values from -6 to 6
- b_mid: bfloat16 [8192, 256], P(('leaf', 'grid'), 'rhs'), may hold values from -6 to 6
- b_root: bfloat16 [4096, 256], P(('leaf', 'grid'), 'rhs'), may hold values from -6 to 6
- inv_leaf: bfloat16 [16384, 4096], P(('leaf', 'grid')), as said below
- inv_mid: bfloat16 [8192, 4096], P(('leaf', 'grid')), as said below
- inv_root: bfloat16 [4096, 4096], P(('leaf', 'grid')), as said below
- up_leaf_mid: bfloat16 [3584, 16384], P('rhs', ('leaf', 'grid')), may hold values from -0.046875 to 0.046875
- up_leaf_root: bfloat16 [3072, 16384], P('rhs', ('leaf', 'grid')), may hold values from -0.046875 to 0.046875
- up_mid_root: bfloat16 [3072, 8192], P(None, ('leaf', 'grid')), may hold values from -0.046875 to 0.046875
- rows_mid: int32 [4, 3584], replicated, may hold values from 0 to 4095, as said below
- rows_root: int32 [4, 3072], replicated, may hold values from 0 to 4095, as said below
- rows_mid_root: int32 [2, 3072], replicated, may hold values from 0 to 4095, as said below
Outputs:
- x_leaf: bfloat16 [16384, 256], P(('leaf', 'grid'), 'rhs')
- x_mid: bfloat16 [8192, 256], P(('leaf', 'grid'), 'rhs')
- x_root: bfloat16 [4096, 256], P(('leaf', 'grid'), 'rhs')
The draws below stay inside these ranges and needn't reach their ends.
Inputs may be any that keep to these rules, and one draw needn't show every extreme that they name: `rows_mid`: each row lists 3584 distinct rows of the parent separator in increasing order. `rows_root`: each row lists 3072 distinct rows of the root in increasing order. `rows_mid_root`: each row lists 3072 distinct rows of the root in increasing order. `inv_leaf`: each 4096 x 4096 block is lower triangular with a positive diagonal. `inv_mid`: lower triangular with a positive diagonal. `inv_root`: lower triangular with a positive diagonal.
All inputs are finite; a program needn't handle non-finite values.
Results may differ from the reference program's by a relative error of at most 0.0085.
Values may be sent and summed in bfloat16 or wider, within the bound.
No kernel may reach another device: no remote copies, remote signals or barrier semaphores. Data moves between devices by JAX's collectives and lax.ppermute only.
A program may use at most 128 MiB of HBM per device.

```python
import jax
import jax.numpy as jnp
from jax import lax

W = 4096
K = 256
LEAVES = 4
MIDS = 2
R_MID = 3584
R_ROOT = 3072


def lower_blocks(key, blocks):
    total_rows = blocks * W
    key_diag, key_off = jax.random.split(key)
    diagonal = jax.random.uniform(key_diag, (total_rows, 1), jnp.float32, 0.6, 1.4)
    spread = jax.random.normal(key_off, (total_rows, W), jnp.float32)
    row_index = lax.broadcasted_iota(jnp.int32, (total_rows, W), 0) % W
    col_index = lax.broadcasted_iota(jnp.int32, (total_rows, W), 1)
    below = jnp.where(col_index < row_index, spread * (0.7 / W ** 0.5), 0.0)
    return below + jnp.where(col_index == row_index, diagonal, 0.0)


def pick_rows(key, lists, length):
    scores = jax.random.randint(key, (lists, W), 0, (1 << 30) // W) * W + lax.broadcasted_iota(jnp.int32, (lists, W), 1)
    chosen = jnp.argsort(scores, axis=1, stable=True)[:, :length]
    return jnp.sort(chosen, axis=1).astype(jnp.int32)


def draw_inv_leaf(key, part):
    return lower_blocks(jax.random.fold_in(key, 1101), LEAVES).astype(jnp.bfloat16)


def draw_inv_mid(key, part):
    return lower_blocks(jax.random.fold_in(key, 1202), MIDS).astype(jnp.bfloat16)


def draw_inv_root(key, part):
    return lower_blocks(jax.random.fold_in(key, 1303), 1).astype(jnp.bfloat16)


def draw_rows_mid(key, part):
    return pick_rows(jax.random.fold_in(key, 2101), LEAVES, R_MID)


def draw_rows_root(key, part):
    return pick_rows(jax.random.fold_in(key, 2202), LEAVES, R_ROOT)


def draw_rows_mid_root(key, part):
    return pick_rows(jax.random.fold_in(key, 2303), MIDS, R_ROOT)


def block_scale(rng, dims, cuts, low, top_value):
    def one(position, blocks):
        steps = jax.random.uniform(jax.random.fold_in(jax.random.fold_in(rng, 6), position), (blocks,), jnp.float32, low / len(cuts), top_value / len(cuts))
        return jnp.repeat(jnp.exp(steps), dims[position] // blocks).reshape((-1,) + (1,) * (len(dims) - position - 1))

    loudness = one(*cuts[0])
    for cut in cuts[1:]:
        loudness = loudness * one(*cut)
    return loudness


def centred(own_key, dims, scale, reach, cuts=(), kind=jnp.bfloat16):
    loudness = block_scale(own_key, dims, cuts, -0.22, 0.18) if cuts else 1.0
    array = jax.random.normal(own_key, dims, jnp.float32) * scale * loudness
    return jnp.minimum(jnp.maximum(array, -reach), reach).astype(kind)


def setup_inputs(seed: int = 0) -> dict:
    arg_keys = jax.random.split(jax.random.key(seed), 13)
    return {
        "b_leaf": centred(arg_keys[0], (LEAVES * W, K), 1.0, 6.0, ((0, 16), (1, 2))),
        "b_mid": centred(arg_keys[1], (MIDS * W, K), 1.0, 6.0, ((0, 16), (1, 2))),
        "b_root": centred(arg_keys[2], (W, K), 1.0, 6.0, ((0, 16), (1, 2))),
        "inv_leaf": draw_inv_leaf(jax.random.fold_in(arg_keys[12], 71), 0),
        "inv_mid": draw_inv_mid(jax.random.fold_in(arg_keys[12], 71), 0),
        "inv_root": draw_inv_root(jax.random.fold_in(arg_keys[12], 71), 0),
        "up_leaf_mid": centred(arg_keys[6], (R_MID, LEAVES * W), (4 * W) ** -0.5, 0.046875, ((0, 2), (1, 16))),
        "up_leaf_root": centred(arg_keys[7], (R_ROOT, LEAVES * W), (4 * W) ** -0.5, 0.046875, ((0, 2), (1, 16))),
        "up_mid_root": centred(arg_keys[8], (R_ROOT, MIDS * W), (4 * W) ** -0.5, 0.046875, ((1, 16),)),
        "rows_mid": draw_rows_mid(jax.random.fold_in(arg_keys[12], 71), 0),
        "rows_root": draw_rows_root(jax.random.fold_in(arg_keys[12], 71), 0),
        "rows_mid_root": draw_rows_mid_root(jax.random.fold_in(arg_keys[12], 71), 0),
    }


def product(left, right):
    return jnp.dot(left, right, preferred_element_type=jnp.float32)


def left_product(left, right):
    return jnp.dot(left.T, right, preferred_element_type=jnp.float32)


def reference(b_leaf, b_mid, b_root, inv_leaf, inv_mid, inv_root, up_leaf_mid, up_leaf_root, up_mid_root, rows_mid, rows_root, rows_mid_root):
    y_leaf = []
    acc_mid = [jnp.zeros((W, K), jnp.float32) for mid_node in range(MIDS)]
    acc_root = jnp.zeros((W, K), jnp.float32)
    for leaf_node in range(LEAVES):
        lower = leaf_node * W
        solved = product(inv_leaf[lower:lower + W], b_leaf[lower:lower + W]).astype(jnp.bfloat16)
        y_leaf.append(solved)
        acc_mid[leaf_node // 2] = acc_mid[leaf_node // 2].at[rows_mid[leaf_node]].add(product(up_leaf_mid[:, lower:lower + W], solved))
        acc_root = acc_root.at[rows_root[leaf_node]].add(product(up_leaf_root[:, lower:lower + W], solved))
    y_mid = []
    for mid_node in range(MIDS):
        lower = mid_node * W
        reduced = (b_mid[lower:lower + W] - acc_mid[mid_node]).astype(jnp.bfloat16)
        solved = product(inv_mid[lower:lower + W], reduced).astype(jnp.bfloat16)
        y_mid.append(solved)
        acc_root = acc_root.at[rows_mid_root[mid_node]].add(product(up_mid_root[:, lower:lower + W], solved))
    reduced_root = (b_root - acc_root).astype(jnp.bfloat16)
    y_root = product(inv_root, reduced_root).astype(jnp.bfloat16)
    x_root = left_product(inv_root, y_root).astype(jnp.bfloat16)
    x_mid = []
    for mid_node in range(MIDS):
        lower = mid_node * W
        update = left_product(up_mid_root[:, lower:lower + W], x_root[rows_mid_root[mid_node]])
        weight = (y_mid[mid_node] - update).astype(jnp.bfloat16)
        x_mid.append(left_product(inv_mid[lower:lower + W], weight).astype(jnp.bfloat16))
    x_leaf = []
    for leaf_node in range(LEAVES):
        lower = leaf_node * W
        update = left_product(up_leaf_mid[:, lower:lower + W], x_mid[leaf_node // 2][rows_mid[leaf_node]])
        update = update + left_product(up_leaf_root[:, lower:lower + W], x_root[rows_root[leaf_node]])
        weight = (y_leaf[leaf_node] - update).astype(jnp.bfloat16)
        x_leaf.append(left_product(inv_leaf[lower:lower + W], weight).astype(jnp.bfloat16))
    return jnp.concatenate(x_leaf, axis=0), jnp.concatenate(x_mid, axis=0), x_root
```

```python
import functools

import jax
import jax.numpy as jnp
from jax import lax
from jax.experimental import pallas as pl
from jax.experimental.pallas import tpu as pltpu
from jax.sharding import PartitionSpec as P


BF16 = jnp.bfloat16
F32 = jnp.float32
PUSH = 256
VMEM_LIMIT = 40 * 2**20


def whole(shape):
    return pl.BlockSpec(shape, lambda *_: (0,) * len(shape))


def bits_of(count):
    return [1 << b for b in range(count.bit_length() - 1)]


def flip(value, axis, mask):
    pairs = [(source, source ^ mask) for source in range(lax.axis_size(axis))]
    return lax.ppermute(value, axis, pairs)


def pick_row(table, index):
    return lax.dynamic_index_in_dim(table, index, 0, keepdims=False)


def gather_order(bits):
    order = [0]
    for bit in bits:
        order = order + [k ^ bit for k in order]
    return order


def scatter_order(bits):
    return gather_order(bits[::-1])


def double_gather(value, axis, bits):
    for bit in bits:
        value = jnp.concatenate([value, flip(value, axis, bit)], axis=0)
    return value


def halve_scatter(value, axis, bits):
    for bit in bits:
        half = value.shape[0] // 2
        got = flip(value[half:].astype(BF16), axis, bit)
        value = value[:half].astype(F32) + got.astype(F32)
    return value


def arrange(starts_ref, base, count, rows, source_ref, target_ref, dtype):
    for i in range(count):
        start = pl.multiple_of(starts_ref[base + i], rows)
        target_ref[i * rows : (i + 1) * rows, :] = source_ref[pl.ds(start, rows), :].astype(dtype)


def restore(starts_ref, base, count, rows, source_ref, target_ref):
    for i in range(count):
        start = pl.multiple_of(starts_ref[base + i], rows)
        target_ref[pl.ds(start, rows), :] = source_ref[i * rows : (i + 1) * rows, :]


def solve_kernel(count, rows, starts_ref, first_ref, second_ref, inv_ref, out_ref, vec_ref):
    @pl.when(pl.program_id(0) == 0)
    def _():
        restore(starts_ref, 0, count, rows, first_ref, vec_ref)
        restore(starts_ref, count, count, rows, second_ref, vec_ref)

    out_ref[...] = jnp.dot(inv_ref[...], vec_ref[...], preferred_element_type=F32).astype(BF16)


def solve(starts, first, second, inverse, rows):
    height, width = inverse.shape
    cols = first.shape[1]
    step = min(256, height)
    count = first.shape[0] // rows
    return pl.pallas_call(
        functools.partial(solve_kernel, count, rows),
        out_shape=jax.ShapeDtypeStruct((height, cols), BF16),
        grid_spec=pltpu.PrefetchScalarGridSpec(
            num_scalar_prefetch=1,
            grid=(height // step,),
            in_specs=[
                whole(first.shape),
                whole(second.shape),
                pl.BlockSpec((step, width), lambda i, s: (i, 0)),
            ],
            out_specs=pl.BlockSpec((step, cols), lambda i, s: (i, 0)),
            scratch_shapes=[pltpu.VMEM((width, cols), BF16)],
        ),
        compiler_params=pltpu.CompilerParams(vmem_limit_bytes=VMEM_LIMIT),
        name="solve",
    )(starts, first, second, inverse)


def place_block(acc_ref, rows_ref, start, update, band):
    length = update.shape[0]
    span = length + band
    listed = rows_ref[:, pl.ds(start, length)] - start
    spot = lax.broadcasted_iota(jnp.int32, (span, length), 0)
    chosen = (spot == listed).astype(F32).astype(BF16)
    acc_ref[pl.ds(start, span), :] += jnp.dot(chosen, update, preferred_element_type=F32)


def push_kernel(steps, parts, band, seeded, arrange_to, starts_ref, *refs):
    blocks = refs[:parts]
    vec_ref, rows_ref = refs[parts : parts + 2]
    rest = refs[parts + 2 :]
    seed_ref = rest[0] if seeded else None
    outs = rest[1 if seeded else 0 : -1]
    acc_ref = rest[-1]
    step = pl.program_id(0)

    @pl.when(step == 0)
    def _():
        if seeded:
            acc_ref[...] = seed_ref[...]
        else:
            acc_ref[...] = jnp.zeros_like(acc_ref)

    for part in range(parts):

        @pl.when((step >= part * steps) & (step < (part + 1) * steps))
        def _(part=part):
            start = starts_ref[part] + (step - part * steps) * PUSH
            start = pl.multiple_of(start, PUSH)
            update = jnp.dot(blocks[part][...], vec_ref[...], preferred_element_type=F32)
            place_block(acc_ref, rows_ref, start, update.astype(BF16), band)

    @pl.when(step == parts * steps - 1)
    def _():
        if arrange_to is None:
            outs[0][...] = acc_ref[...]
        else:
            count, rows = arrange_to
            arrange(starts_ref, parts, count, rows, acc_ref, outs[0], BF16)
            arrange(starts_ref, parts + count, count, rows, acc_ref, outs[1], BF16)


def push(starts, blocks, vec, row_list, node_width, seed=None, arrange_to=None):
    parts = len(blocks)
    height, depth = blocks[0].shape
    cols = vec.shape[1]
    listed = row_list.shape[0]
    steps = height // PUSH
    block_spec = [
        pl.BlockSpec(
            (PUSH, depth),
            lambda i, s, part=part: (jnp.clip(i - part * steps, 0, steps - 1), 0),
        )
        for part in range(parts)
    ]
    if arrange_to is None:
        out_shape = (jax.ShapeDtypeStruct((node_width, cols), F32),)
    else:
        shape = (arrange_to[0] * arrange_to[1], cols)
        out_shape = (jax.ShapeDtypeStruct(shape, BF16),) * 2
    seeds = [] if seed is None else [seed]
    return pl.pallas_call(
        functools.partial(
            push_kernel, steps, parts, node_width - listed, seed is not None, arrange_to
        ),
        out_shape=out_shape,
        grid_spec=pltpu.PrefetchScalarGridSpec(
            num_scalar_prefetch=1,
            grid=(parts * steps,),
            in_specs=block_spec
            + [whole(vec.shape), whole((1, listed))]
            + [whole(s.shape) for s in seeds],
            out_specs=tuple(whole(o.shape) for o in out_shape),
            scratch_shapes=[pltpu.VMEM((node_width, cols), F32)],
        ),
        compiler_params=pltpu.CompilerParams(vmem_limit_bytes=VMEM_LIMIT),
        name="push",
    )(starts, *blocks, vec, row_list[None, :], *seeds)


def pull_kernel(steps, parts, count, rows, band, starts_ref, *refs):
    blocks = refs[:parts]
    first_ref, second_ref, lanes_ref, out_ref, vec_ref, acc_ref = refs[parts:]
    step = pl.program_id(0)

    @pl.when(step == 0)
    def _():
        restore(starts_ref, parts, count, rows, first_ref, vec_ref)
        restore(starts_ref, parts + count, count, rows, second_ref, vec_ref)
        acc_ref[...] = jnp.zeros_like(acc_ref)

    for part in range(parts):

        @pl.when((step >= part * steps) & (step < (part + 1) * steps))
        def _(part=part):
            start = starts_ref[part] + (step - part * steps) * PUSH
            start = pl.multiple_of(start, PUSH)
            span = PUSH + band
            listed = lanes_ref[pl.ds(start, PUSH), :] - start
            spot = lax.broadcasted_iota(jnp.int32, (PUSH, 128), 1)
            chosen = jnp.concatenate(
                [
                    (spot + off == listed).astype(F32).astype(BF16)
                    for off in range(0, span, 128)
                ],
                axis=1,
            )
            picked = jnp.dot(chosen, vec_ref[pl.ds(start, span), :], preferred_element_type=F32)
            acc_ref[...] += jnp.dot(
                picked.T.astype(BF16), blocks[part][...], preferred_element_type=F32
            )

    @pl.when(step == parts * steps - 1)
    def _():
        out_ref[...] = acc_ref[...]


def pull(starts, blocks, first, second, lanes, node_width, rows):
    parts = len(blocks)
    height, depth = blocks[0].shape
    cols = first.shape[1]
    listed = lanes.shape[0]
    steps = height // PUSH
    count = first.shape[0] // rows
    block_spec = [
        pl.BlockSpec(
            (PUSH, depth),
            lambda i, s, part=part: (jnp.clip(i - part * steps, 0, steps - 1), 0),
        )
        for part in range(parts)
    ]
    return pl.pallas_call(
        functools.partial(pull_kernel, steps, parts, count, rows, node_width - listed),
        out_shape=jax.ShapeDtypeStruct((cols, depth), F32),
        grid_spec=pltpu.PrefetchScalarGridSpec(
            num_scalar_prefetch=1,
            grid=(parts * steps,),
            in_specs=block_spec
            + [whole(first.shape), whole(second.shape), whole(lanes.shape)],
            out_specs=whole((cols, depth)),
            scratch_shapes=[
                pltpu.VMEM((node_width, cols), BF16),
                pltpu.VMEM((cols, depth), F32),
            ],
        ),
        compiler_params=pltpu.CompilerParams(vmem_limit_bytes=VMEM_LIMIT),
        name="pull",
    )(starts, *blocks, first, second, lanes)


def back_kernel(updates, count, rows, starts_ref, y_ref, *refs):
    pulled = refs[:updates]
    inv_ref, first_ref, second_ref, weight_ref, out_ref = refs[updates:]
    step = pl.program_id(0)
    width = inv_ref.shape[1]

    @pl.when(step == 0)
    def _():
        weight = y_ref[...].astype(F32).T
        if updates:
            total = pulled[0][...]
            for other in pulled[1:]:
                total = total + other[...]
            weight = weight - total
        weight_ref[...] = weight.astype(BF16)

    product = jnp.dot(weight_ref[...], inv_ref[...], preferred_element_type=F32)
    start = pl.multiple_of(step * width, width)
    out_ref[pl.ds(start, width), :] = product.T

    @pl.when(step == pl.num_programs(0) - 1)
    def _():
        arrange(starts_ref, 0, count, rows, out_ref, first_ref, BF16)
        arrange(starts_ref, count, count, rows, out_ref, second_ref, BF16)


def back(starts, y, pulled, inverse, count, rows):
    height, width = inverse.shape
    cols = y.shape[1]
    step = min(width, 1024)
    out = jax.ShapeDtypeStruct((count * rows, cols), BF16)
    return pl.pallas_call(
        functools.partial(back_kernel, len(pulled), count, rows),
        out_shape=(out, out),
        grid_spec=pltpu.PrefetchScalarGridSpec(
            num_scalar_prefetch=1,
            grid=(width // step,),
            in_specs=[whole(y.shape)]
            + [whole(p.shape) for p in pulled]
            + [pl.BlockSpec((height, step), lambda i, s: (0, i))],
            out_specs=(whole(out.shape), whole(out.shape)),
            scratch_shapes=[
                pltpu.VMEM((cols, height), BF16),
                pltpu.VMEM((width, cols), F32),
            ],
        ),
        compiler_params=pltpu.CompilerParams(vmem_limit_bytes=VMEM_LIMIT),
        name="back",
    )(starts, y, *pulled, inverse)


def per_device(
    b_leaf,
    b_mid,
    b_root,
    inv_leaf,
    inv_mid,
    inv_root,
    up_leaf_mid,
    up_leaf_root,
    up_mid_root,
    rows_mid,
    rows_root,
    rows_mid_root,
):
    leaf_id = lax.axis_index("leaf")
    grid_id = lax.axis_index("grid")
    rhs_id = lax.axis_index("rhs")
    leaf_count = lax.axis_size("leaf")
    grid_count = lax.axis_size("grid")
    width = inv_leaf.shape[1]
    cols = b_leaf.shape[1]
    n_leaf, n_mid, n_root = b_leaf.shape[0], b_mid.shape[0], b_root.shape[0]
    sibling = leaf_id % 2

    own_rows_mid = pick_row(rows_mid, leaf_id)
    own_rows_root = pick_row(rows_root, leaf_id)
    parent_rows_root = pick_row(rows_mid_root, leaf_id // 2)
    lanes_mid = jnp.broadcast_to(own_rows_mid[:, None], (own_rows_mid.shape[0], cols))
    lanes_root = jnp.broadcast_to(own_rows_root[:, None], (own_rows_root.shape[0], cols))
    lanes_parent = jnp.broadcast_to(parent_rows_root[:, None], (parent_rows_root.shape[0], cols))

    far_leaf_mid = flip(up_leaf_mid, "rhs", 1)
    far_leaf_root = flip(up_leaf_root, "rhs", 1)

    bits = bits_of(grid_count)
    back_bits = bits[::-1]
    deep = bits_of(leaf_count)

    def table(values):
        return jnp.stack([jnp.asarray(v, jnp.int32) for v in values])

    def leaf_starts(order, half):
        return [(grid_id ^ k) * n_leaf + half * (n_leaf // 2) for k in order]

    def mid_starts(order, far):
        side = sibling ^ far
        return [(side * grid_count + (grid_id ^ k)) * n_mid for k in order]

    low = gather_order(deep[:-1])
    high = [k ^ deep[-1] for k in low]

    def root_starts(order, far):
        return [
            ((leaf_id ^ m) * grid_count + (grid_id ^ k)) * n_root
            for k in order
            for m in (high if far else low)
        ]

    g_first, g_second = gather_order(bits), gather_order(back_bits)
    s_first, s_second = scatter_order(bits), scatter_order(back_bits)
    offsets_mid = [rhs_id * up_leaf_mid.shape[0], (1 - rhs_id) * up_leaf_mid.shape[0]]
    offsets_root = [rhs_id * up_leaf_root.shape[0], (1 - rhs_id) * up_leaf_root.shape[0]]
    leaf_gather = leaf_starts(g_first, 0) + leaf_starts(g_second, 1)
    leaf_scatter = leaf_starts(s_first, 0) + leaf_starts(s_second, 1)
    mid_gather = mid_starts(g_first, 0) + mid_starts(g_second, 1)
    mid_scatter = mid_starts(s_first, 0) + mid_starts(s_second, 1)
    root_gather = root_starts(g_first, 0) + root_starts(g_second, 1)
    root_scatter = root_starts(s_first, 0) + root_starts(s_second, 1)

    def gather_pair(first, second):
        return double_gather(first, "grid", bits), double_gather(second, "grid", back_bits)

    def scatter_pair(first, second):
        return halve_scatter(first, "grid", bits), halve_scatter(second, "grid", back_bits)

    def scatter_mid(first, second):
        own, far = scatter_pair(first, second)
        return own + flip(far.astype(BF16), "leaf", 1).astype(F32)

    def scatter_root(first, second):
        near, far = scatter_pair(first, second)
        total = near + flip(far.astype(BF16), "leaf", deep[-1]).astype(F32)
        return halve_scatter(total, "leaf", deep[:-1][::-1])

    def gather_root(value):
        near = double_gather(value, "leaf", deep[:-1])
        return gather_pair(near, flip(near, "leaf", deep[-1]))

    half = n_leaf // 2
    b_first, b_second = gather_pair(b_leaf[:half], b_leaf[half:])
    y_leaf = solve(table(leaf_gather), b_first, b_second, inv_leaf, half)
    sent = push(
        table(offsets_mid + mid_scatter),
        (up_leaf_mid, far_leaf_mid),
        y_leaf,
        own_rows_mid,
        width,
        arrange_to=(grid_count, n_mid),
    )
    acc_mid = scatter_mid(*sent)
    (root_seed,) = push(
        table(offsets_root), (up_leaf_root, far_leaf_root), y_leaf, own_rows_root, width
    )
    reduced_mid = (b_mid - acc_mid).astype(BF16)
    v_first, v_second = gather_pair(reduced_mid, flip(reduced_mid, "leaf", 1))
    y_mid = solve(table(mid_gather), v_first, v_second, inv_mid, n_mid)
    sent = push(
        table([0] + root_scatter),
        (up_mid_root,),
        y_mid,
        parent_rows_root,
        width,
        seed=root_seed,
        arrange_to=(grid_count * len(low), n_root),
    )
    acc_root = scatter_root(*sent)
    reduced_root = (b_root - acc_root).astype(BF16)

    r_first, r_second = gather_root(reduced_root)
    y_root = solve(table(root_gather), r_first, r_second, inv_root, n_root)
    sent = back(table(root_scatter), y_root, (), inv_root, grid_count * len(low), n_root)
    x_root = scatter_root(*sent).astype(BF16)
    r_first, r_second = gather_root(x_root)

    pulled = pull(
        table([0] + root_gather), (up_mid_root,), r_first, r_second, lanes_parent, width, n_root
    )
    sent = back(table(mid_scatter), y_mid, (pulled,), inv_mid, grid_count, n_mid)
    x_mid = scatter_mid(*sent).astype(BF16)
    pulled_root = pull(
        table(offsets_root + root_gather),
        (up_leaf_root, far_leaf_root),
        r_first,
        r_second,
        lanes_root,
        width,
        n_root,
    )
    v_first, v_second = gather_pair(x_mid, flip(x_mid, "leaf", 1))
    pulled_mid = pull(
        table(offsets_mid + mid_gather),
        (up_leaf_mid, far_leaf_mid),
        v_first,
        v_second,
        lanes_mid,
        width,
        n_mid,
    )
    sent = back(
        table(leaf_scatter), y_leaf, (pulled_mid, pulled_root), inv_leaf, grid_count, half
    )
    x_first, x_second = scatter_pair(*sent)
    x_leaf = jnp.concatenate([x_first, x_second], axis=0).astype(BF16)
    return (x_leaf, x_mid, x_root)


def solution(mesh):
    split = ("leaf", "grid")
    vector = P(split, "rhs")
    placed = (vector,) * 3 + (P(split, None),) * 3
    placed += (P("rhs", split), P("rhs", split), P(None, split), P(), P(), P())
    return jax.shard_map(
        per_device,
        mesh=mesh,
        in_specs=placed,
        out_specs=(vector,) * 3,
        check_vma=False,
    )
```
